128 devices in a mesh: replica: 8 (over z, y_hi), tensor: 16 (over x, y_lo, core).
Axes of the slice: x: 4, y: 4 (y_hi: 2, y_lo: 2; y = y_hi * 2 + y_lo), z: 4, core: 2. Of those that a mesh axis runs over, the one named last changes fastest.
Arguments:
- hidden_input: bfloat16 [2560, 2, 8192], P('replica', None, 'tensor'), may hold values from -200 to 200
- input_norm_gain: bfloat16 [8192], replicated, may hold values from 0.099609375 to 1.8984375
- merged_weight: bfloat16 [8192, 6144], P(None, 'tensor'), may hold values from -0.0625 to 0.0625
- output_weight: bfloat16 [4096, 8192], P('tensor'), may hold values from -0.375 to 0.375
- adapter_down: bfloat16 [256, 16, 8192], P('replica', None, 'tensor'), may hold values from -0.0625 to 0.0625
- adapter_up: bfloat16 [256, 16, 6144], P('replica', None, 'tensor'), may hold values from -0.75 to 0.75
- request_adapter: int32 [2560], replicated, may hold values from 0 to 255
- key_value_cache: bfloat16 [20480, 16, 2048], P(('replica', 'tensor')), may hold values from -1000 to 1000
- block_table: int32 [2560, 8], P(('replica', 'tensor')), may hold values from 0 to 159, as said below
- cache_length: int32 [2560], P(('replica', 'tensor')), may hold values from 1 to 128, as said below
- partner: int32 [8, 16], replicated, may hold values from 0 to 7, as said below
- moving: int32 [2560], P(('replica', 'tensor')), may hold values from 0 to 1, as said below
Outputs:
- attn_out: bfloat16 [2560, 2, 8192], P('replica', None, 'tensor')
- arrived_kv: bfloat16 [256, 128, 2048], P(('replica', 'tensor'))
The draws below stay inside these ranges and needn't reach their ends.
Inputs may be any that keep to these rules, and one draw needn't show every extreme that they name: `block_table`: the rows of one device (the 20 home slots of one replica and one tensor index) hold every block index of 0 to 159 exactly once. `cache_length`: among the 20 requests of one device one has all 128 positions cached. partner[r, k] = r XOR m_k for one m_k of 1 to 7 for each tensor index k, the same for every replica. Slot s of replica r moves exactly when slot s of replica partner[r, s // 20] does. Each device's 20 slots hold 1 to 2 moving ones, and some device holds 2.
All inputs are finite; a program needn't handle non-finite values.
Results may differ from the reference program's by a relative error of at most 0.035.
Values may be sent and summed in bfloat16 or wider, within the bound.
No kernel may reach another device: no remote copies, remote signals or barrier semaphores. Data moves between devices by JAX's collectives and lax.ppermute only.
A program may use at most 256 MiB of HBM per device.

```python
import math
import jax
import jax.numpy as jnp
import numpy as np
from jax import lax

EMBED_WIDTH = 8192
QUERY_HEADS = 32
KEY_VALUE_HEADS = 8
HEAD_SIZE = 128
ADAPTER_RANK = 16
ADAPTER_TOTAL = 256
FRESH_TOKENS = 2
BLK = 16
MAXB = 8
MIG_DEV = 2
REQUESTS_LOCAL = 20
MERGED_COLUMNS = 6144
LMAX = 128
REPLICAS = 8
TENSORS = 16
B = 320
REQUEST_TOTAL = 2560
NBLK_DEV = 160
POOL = 20480
N_TENSOR = 16


def draw_hidden_input(key, part):
    values = jnp.clip(jax.random.normal(key, (REQUEST_TOTAL, FRESH_TOKENS, EMBED_WIDTH), jnp.float32), -6.0, 6.0)
    return values.astype(jnp.bfloat16)


def draw_key_value_cache(key, part):
    track_count = 2 * KEY_VALUE_HEADS * HEAD_SIZE
    shape_all = (POOL, BLK, track_count)
    values = jax.random.normal(key, shape_all, jnp.float32)
    return jnp.clip(values, -1000.0, 1000.0).astype(jnp.bfloat16)


def draw_block_table(key, part):
    device_keys = jax.random.split(key, REPLICAS * TENSORS)
    orders = jax.vmap(lambda single_key: jax.random.permutation(single_key, NBLK_DEV))(device_keys)
    return orders.reshape(REQUEST_TOTAL, MAXB).astype(jnp.int32)


def draw_cache_length(key, part):
    lengths = jax.random.randint(key, (REPLICAS * TENSORS, REQUESTS_LOCAL), 1, LMAX + 1)
    full_at = jax.random.randint(jax.random.fold_in(key, 21), (REPLICAS * TENSORS, 1), 0, REQUESTS_LOCAL)
    lengths = jnp.where(jnp.arange(REQUESTS_LOCAL, dtype=jnp.int32)[None, :] == full_at, LMAX, lengths)
    return lengths.reshape(REQUEST_TOTAL).astype(jnp.int32)


def pair_mask(key):
    return jax.random.randint(jax.random.fold_in(key, 11), (TENSORS,), 1, REPLICAS).astype(jnp.int32)


def draw_partner(key, part):
    flip_bits = pair_mask(key)
    replica_ids = jnp.arange(REPLICAS, dtype=jnp.int32)
    return jnp.bitwise_xor(replica_ids[:, None], flip_bits[None, :]).astype(jnp.int32)


def draw_moving(key, part):
    flip_bits = pair_mask(key)
    counts = jax.random.randint(jax.random.fold_in(key, 12), (REPLICAS, TENSORS), 1, MIG_DEV + 1)
    full_at = jax.random.randint(jax.random.fold_in(key, 13), (REPLICAS, 1), 0, TENSORS)
    counts = jnp.where(jnp.arange(TENSORS, dtype=jnp.int32)[None, :] == full_at, MIG_DEV, counts)
    device_keys = jax.random.split(jax.random.fold_in(key, 14), REPLICAS * TENSORS)
    orders = jax.vmap(lambda single_key: jax.random.permutation(single_key, REQUESTS_LOCAL))(device_keys)
    ranks = jnp.argsort(orders, axis=-1).reshape(REPLICAS, TENSORS, REQUESTS_LOCAL)
    chosen = (ranks < counts[:, :, None]).astype(jnp.int32)
    replica_ids = jnp.arange(REPLICAS, dtype=jnp.int32)
    lower = jnp.minimum(replica_ids[:, None], jnp.bitwise_xor(replica_ids[:, None], flip_bits[None, :]))
    tensor_ids = jnp.arange(TENSORS, dtype=jnp.int32)[None, :]
    return chosen[lower, tensor_ids].reshape(REQUEST_TOTAL).astype(jnp.int32)


def place_ends(values, own_key, smallest, largest):
    shape = values.shape
    spot = [jax.random.randint(jax.random.fold_in(own_key, axis), (), 0, shape[axis]) for axis in range(len(shape))]
    values = values.at[tuple(spot)].set(smallest)
    longest = shape.index(max(shape))
    spot[longest] = (spot[longest] + 1) % shape[longest]
    return values.at[tuple(spot)].set(largest)


def block_scale(rng, dims, pieces, smallest, top_value):
    loudness = 1.0
    for position, blocks in pieces:
        steps = jax.random.uniform(jax.random.fold_in(jax.random.fold_in(rng, 6), position), (blocks,), jnp.float32, smallest / len(pieces), top_value / len(pieces))
        loudness = loudness * jnp.repeat(jnp.exp(steps), dims[position] // blocks).reshape((-1,) + (1,) * (len(dims) - 1 - position))
    return loudness


def rank_table(amount, slope):
    weights = [(1 << 20) // math.isqrt(rank ** slope) + 1 for rank in range(1, amount + 1)]
    width = 1 + sum(weights) // (1 << 30)
    return np.cumsum(np.array([max(1, weight // width) for weight in weights]))


def ranked_ids(rng, shape, amount, slope):
    grid = rank_table(amount, slope)
    lot = jax.random.randint(jax.random.fold_in(rng, 1), shape, 0, int(grid[amount - 1]))
    standing = jnp.searchsorted(jnp.asarray(grid, jnp.int32), lot, side="right")
    return jax.random.permutation(jax.random.fold_in(rng, 2), amount)[standing].astype(jnp.int32)


def bell_draw(key, shape, scale, bound, pieces=(), kind=jnp.bfloat16):
    array = jax.random.normal(key, shape, jnp.float32) * scale
    if len(pieces) > 0:
        array = block_scale(key, shape, pieces, -0.22, 0.18) * array
    return jnp.clip(array, min=-bound, max=bound).astype(kind)


def setup_inputs(seed: int = 0) -> dict:
    streams_of = jax.random.split(jax.random.key(seed), 13)
    return {
        "hidden_input": draw_hidden_input(jax.random.fold_in(streams_of[12], 71), 0),
        "input_norm_gain": jnp.clip(1.0 + 0.18 * jax.random.normal(streams_of[1], (EMBED_WIDTH,), jnp.float32), 0.099609375, 1.8984375).astype(jnp.bfloat16),
        "merged_weight": bell_draw(streams_of[2], (EMBED_WIDTH, MERGED_COLUMNS), EMBED_WIDTH ** -0.5, 0.0625, ((1, 16),)),
        "output_weight": bell_draw(streams_of[3], (QUERY_HEADS * HEAD_SIZE, EMBED_WIDTH), (QUERY_HEADS * HEAD_SIZE // 16) ** -0.5, 0.375, ((0, 16),)),
        "adapter_down": bell_draw(streams_of[4], (ADAPTER_TOTAL, ADAPTER_RANK, EMBED_WIDTH), EMBED_WIDTH ** -0.5, 0.0625, ((0, 8), (2, 16))),
        "adapter_up": bell_draw(streams_of[5], (ADAPTER_TOTAL, ADAPTER_RANK, MERGED_COLUMNS), (4 * ADAPTER_RANK) ** -0.5, 0.75, ((0, 8), (2, 16))),
        "request_adapter": place_ends(ranked_ids(streams_of[6], (REQUEST_TOTAL,), ADAPTER_TOTAL, 2), jax.random.fold_in(streams_of[6], 3), 0, ADAPTER_TOTAL - 1).astype(jnp.int32),
        "key_value_cache": draw_key_value_cache(jax.random.fold_in(streams_of[12], 71), 0),
        "block_table": draw_block_table(jax.random.fold_in(streams_of[12], 71), 0),
        "cache_length": draw_cache_length(jax.random.fold_in(streams_of[12], 71), 0),
        "partner": draw_partner(jax.random.fold_in(streams_of[12], 71), 0),
        "moving": draw_moving(jax.random.fold_in(streams_of[12], 71), 0),
    }


theta_base = 500000.0
norm_eps = 1e-05
adapter_scale = 2.0

def rotate(vectors, positions):
    track_count = vectors.shape[-1]
    half_width = track_count // 2
    frequency = jnp.power(jnp.float32(theta_base), -jnp.arange(half_width, dtype=jnp.float32) / half_width)
    angles = positions.astype(jnp.float32)[..., None] * frequency
    cosine = jnp.cos(angles)
    sine_part = jnp.sin(angles)
    first_half = vectors[..., :half_width].astype(jnp.float32)
    second = vectors[..., half_width:].astype(jnp.float32)
    joined = jnp.concatenate([first_half * cosine - second * sine_part, second * cosine + first_half * sine_part], axis=-1)
    return joined.astype(jnp.bfloat16)

def new_entries(projected_rows, lengths):
    item_count = projected_rows.shape[0]
    fresh_tokens = projected_rows.shape[1]
    query_columns = QUERY_HEADS * HEAD_SIZE
    key_columns = KEY_VALUE_HEADS * HEAD_SIZE
    fresh_keys = projected_rows[:, :, query_columns:query_columns + key_columns].reshape(item_count, fresh_tokens, KEY_VALUE_HEADS, HEAD_SIZE)
    offsets = jnp.arange(fresh_tokens, dtype=jnp.int32)
    positions = lengths[:, None] + offsets[None, :]
    rotated = rotate(fresh_keys, positions[:, :, None]).reshape(item_count, fresh_tokens, key_columns)
    fresh_values = projected_rows[:, :, query_columns + key_columns:]
    return jnp.concatenate([rotated, fresh_values], axis=-1)

def append_cache(key_value_blocks, entries, lengths, live):
    span = key_value_blocks.shape[1]
    places = jnp.arange(span, dtype=jnp.int32)[None, :]
    kept = jnp.where((places < lengths[:, None])[:, :, None], key_value_blocks, jnp.zeros((), key_value_blocks.dtype))
    for offset in range(entries.shape[1]):
        written = (places == lengths[:, None] + offset)[:, :, None]
        kept = jnp.where(written, entries[:, offset][:, None, :], kept)
    return jnp.where(live[:, None, None], kept, jnp.zeros((), kept.dtype))

def attend(projected_rows, key_value_blocks, lengths):
    item_count = projected_rows.shape[0]
    fresh_tokens = projected_rows.shape[1]
    head_sharing = QUERY_HEADS // KEY_VALUE_HEADS
    cache_extent = key_value_blocks.shape[1]
    query_columns = QUERY_HEADS * HEAD_SIZE
    key_columns = KEY_VALUE_HEADS * HEAD_SIZE
    query_rows = projected_rows[:, :, :query_columns].reshape(item_count, fresh_tokens, KEY_VALUE_HEADS, head_sharing, HEAD_SIZE)
    fresh_keys = projected_rows[:, :, query_columns:query_columns + key_columns].reshape(item_count, fresh_tokens, KEY_VALUE_HEADS, HEAD_SIZE)
    fresh_values = projected_rows[:, :, query_columns + key_columns:].reshape(item_count, fresh_tokens, KEY_VALUE_HEADS, HEAD_SIZE).astype(jnp.float32)
    offsets = jnp.arange(fresh_tokens, dtype=jnp.int32)
    positions = lengths[:, None] + offsets[None, :]
    query_rows = rotate(query_rows, positions[:, :, None, None]).astype(jnp.float32)
    fresh_keys = rotate(fresh_keys, positions[:, :, None]).astype(jnp.float32)
    prior_keys = key_value_blocks[:, :, :key_columns].reshape(item_count, cache_extent, KEY_VALUE_HEADS, HEAD_SIZE).astype(jnp.float32)
    prior_values = key_value_blocks[:, :, key_columns:].reshape(item_count, cache_extent, KEY_VALUE_HEADS, HEAD_SIZE).astype(jnp.float32)
    scaling = HEAD_SIZE ** (-0.5)
    old_scores = jnp.einsum('nthgd,nlhd->nthgl', query_rows, prior_keys) * scaling
    new_scores = jnp.einsum('nthgd,nshd->nthgs', query_rows, fresh_keys) * scaling
    old_valid = jnp.arange(cache_extent, dtype=jnp.int32)[None, :] < lengths[:, None]
    new_valid = offsets[None, :] <= offsets[:, None]
    old_scores = jnp.where(old_valid[:, None, None, None, :], old_scores, -jnp.inf)
    new_scores = jnp.where(new_valid[None, :, None, None, :], new_scores, -jnp.inf)
    highest = jnp.maximum(lax.optimization_barrier(jnp.max(old_scores, axis=-1)), lax.optimization_barrier(jnp.max(new_scores, axis=-1)))
    old_exp = jnp.exp(old_scores - highest[..., None])
    new_exp = jnp.exp(new_scores - highest[..., None])
    totals = lax.optimization_barrier(jnp.sum(old_exp, axis=-1)) + lax.optimization_barrier(jnp.sum(new_exp, axis=-1))
    old_weights = (old_exp / totals[..., None]).astype(jnp.bfloat16).astype(jnp.float32)
    new_weights = (new_exp / totals[..., None]).astype(jnp.bfloat16).astype(jnp.float32)
    mixed = jnp.einsum('nthgl,nlhd->nthgd', old_weights, prior_values) + jnp.einsum('nthgs,nshd->nthgd', new_weights, fresh_values)
    return mixed.reshape(item_count, fresh_tokens, QUERY_HEADS * HEAD_SIZE).astype(jnp.bfloat16)

def reference(hidden_input, input_norm_gain, merged_weight, output_weight, adapter_down, adapter_up, request_adapter, key_value_cache, block_table, cache_length, partner, moving):
    hidden_f = hidden_input.astype(jnp.float32)
    mean_square = lax.optimization_barrier(jnp.mean(hidden_f * hidden_f, axis=-1, keepdims=True))
    normed_hidden = (hidden_f * lax.rsqrt(mean_square + norm_eps) * input_norm_gain.astype(jnp.float32)).astype(jnp.bfloat16)
    base_projection = jnp.dot(normed_hidden.reshape(-1, EMBED_WIDTH), merged_weight, preferred_element_type=jnp.float32).reshape(REQUEST_TOTAL, FRESH_TOKENS, MERGED_COLUMNS)
    group_total = REQUEST_TOTAL // REQUESTS_LOCAL

    def adapter_block(input_values):
        rows_block, block_index_list = input_values
        down_weight_rows = adapter_down[block_index_list].astype(jnp.float32)
        shrink = jnp.einsum('bnd,brd->bnr', rows_block.astype(jnp.float32), down_weight_rows)
        shrink_low = lax.optimization_barrier(shrink.astype(jnp.bfloat16))
        up_weight_rows = adapter_up[block_index_list].astype(jnp.float32)
        return jnp.einsum('bnr,brc->bnc', shrink_low.astype(jnp.float32), up_weight_rows)
    widen_step = lax.map(adapter_block, (normed_hidden.reshape(group_total, REQUESTS_LOCAL, FRESH_TOKENS, EMBED_WIDTH), request_adapter.reshape(group_total, REQUESTS_LOCAL)))
    projected_rows = (base_projection + adapter_scale * widen_step.reshape(REQUEST_TOTAL, FRESH_TOKENS, MERGED_COLUMNS)).astype(jnp.bfloat16)
    slots = jnp.arange(REQUEST_TOTAL, dtype=jnp.int32)
    replica_of = slots // B
    tensor_of = slots % B // REQUESTS_LOCAL
    home = jnp.where(moving == 1, partner[replica_of, tensor_of], replica_of).astype(jnp.int32)
    home_slot = (home * B + slots % B).astype(jnp.int32)
    block_ids = ((home_slot // REQUESTS_LOCAL)[:, None] * NBLK_DEV + block_table[home_slot]).astype(jnp.int32)
    track_count = key_value_cache.shape[2]

    def attend_block(input_values):
        proj_block, block_index_list, lens_block, moves_block = input_values
        key_value_blocks = key_value_cache[block_index_list].reshape(REQUESTS_LOCAL, LMAX, track_count)
        mixed = attend(proj_block, key_value_blocks, lens_block)
        picked = jnp.argsort(1 - moves_block, stable=True)[:MIG_DEV].astype(jnp.int32)
        entries = new_entries(proj_block[picked], lens_block[picked])
        arrived = append_cache(key_value_blocks[picked], entries, lens_block[picked], moves_block[picked] == 1)
        return (mixed, arrived)
    attended, arrived = lax.map(attend_block, (projected_rows.reshape(group_total, REQUESTS_LOCAL, FRESH_TOKENS, MERGED_COLUMNS), block_ids.reshape(group_total, REQUESTS_LOCAL, MAXB), cache_length.reshape(group_total, REQUESTS_LOCAL), moving.reshape(group_total, REQUESTS_LOCAL)))
    attended = attended.reshape(REQUEST_TOTAL, FRESH_TOKENS, QUERY_HEADS * HEAD_SIZE)
    arrived = arrived.reshape(group_total * MIG_DEV, LMAX, track_count)
    shard_cols = QUERY_HEADS * HEAD_SIZE // N_TENSOR

    def out_shard(totals, shard):
        columns = lax.dynamic_slice_in_dim(attended, shard * shard_cols, shard_cols, 2)
        weights = lax.dynamic_slice_in_dim(output_weight, shard * shard_cols, shard_cols, 0)
        partial_value = jnp.dot(columns.reshape(-1, shard_cols), weights, preferred_element_type=jnp.float32).astype(jnp.bfloat16)
        partial_value = lax.optimization_barrier(partial_value)
        return (totals + partial_value.astype(jnp.float32), None)
    totals, unused = lax.scan(out_shard, jnp.zeros((REQUEST_TOTAL * FRESH_TOKENS, EMBED_WIDTH), jnp.float32), jnp.arange(N_TENSOR, dtype=jnp.int32))
    return (totals.reshape(REQUEST_TOTAL, FRESH_TOKENS, EMBED_WIDTH).astype(jnp.bfloat16), arrived)
```

```python
import functools

import jax
import jax.numpy as jnp
from jax import lax
from jax.experimental import pallas as pl
from jax.experimental.pallas import tpu as pltpu
from jax.sharding import Mesh
from jax.sharding import PartitionSpec as P


QUERY_HEADS = 32
KEY_VALUE_HEADS = 8
HEAD_SIZE = 128
MIG_DEV = 2
REPLICA = ("z", "h")
PLANE = ("x", "l")
TENSOR = ("x", "l", "c")
REPLICA_TENSOR = REPLICA + TENSOR
NEW_ROWS = 16

theta_base = 500000.0
norm_eps = 1e-05
adapter_scale = 2.0

f32 = jnp.float32
bf16 = jnp.bfloat16

SMEM = pl.BlockSpec(memory_space=pltpu.SMEM)
VMEM = pl.BlockSpec(memory_space=pltpu.VMEM)
ANY = pl.BlockSpec(memory_space=pl.ANY)


def params(mib):
    return pltpu.CompilerParams(vmem_limit_bytes=mib << 20)


def shift(block, axis, step):
    count = lax.axis_size(axis)
    return lax.ppermute(block, axis, [(i, (i + step) % count) for i in range(count)])


def swap_bit(block, axis, bit):
    count = lax.axis_size(axis)
    return lax.ppermute(block, axis, [(i, i ^ (1 << bit)) for i in range(count)])


OFFSETS = ((0, 0), (0, 1), (3, 0), (1, 0), (3, 1), (1, 1), (2, 0), (2, 1))


def ring_gather(own, ring, pair):
    other = shift(own, pair, 1)
    behind = shift(own, ring, 1)
    ahead = shift(own, ring, -1)
    other_behind = shift(other, ring, 1)
    other_ahead = shift(other, ring, -1)
    far = shift(behind, ring, 1)
    other_far = shift(other_ahead, ring, -1)
    return [own, other, behind, ahead, other_behind, other_ahead, far, other_far]


def ring_places(ring, pair):
    a = lax.axis_index(ring)
    b = lax.axis_index(pair)
    count = lax.axis_size(ring)
    ring_offset = jnp.array([o for o, _ in OFFSETS], jnp.int32)
    flip = jnp.array([f for _, f in OFFSETS], jnp.int32)
    return ((a + ring_offset) % count) * 2 + (b ^ flip)


def shrink_kernel(count, base_ref, ids_ref, hidden_ref, *refs):
    down_refs = refs[:count]
    start_ref = refs[count] if len(refs) > count + 1 else None
    out_ref = refs[-1]
    rank, rows = out_ref.shape
    hidden = hidden_ref[...]
    ids = ids_ref[...]
    total = start_ref[...] if start_ref is not None else jnp.zeros((rank, rows), f32)
    step = 128
    held = step // rank
    for index in range(count):
        relative = ids - base_ref[index]
        for begin in range(0, down_refs[index].shape[0], step):
            products = lax.dot_general(
                down_refs[index][begin : begin + step, :],
                hidden,
                (((1,), (1,)), ((), ())),
                preferred_element_type=f32,
            )
            owner = lax.broadcasted_iota(jnp.int32, (step, rows), 0) // rank + begin // rank
            chosen = jnp.where(owner == relative, products, 0.0)
            for part in range(held):
                total = total + chosen[part * rank : (part + 1) * rank, :]
    out_ref[...] = total


def shrink(base, ids_row, hidden, downs, start=None):
    count = len(downs)
    rank = 16
    extra = () if start is None else (start,)
    return pl.pallas_call(
        functools.partial(shrink_kernel, count),
        out_shape=jax.ShapeDtypeStruct((rank, hidden.shape[0]), f32),
        in_specs=[SMEM] + [VMEM] * (2 + count + len(extra)),
        out_specs=VMEM,
        compiler_params=params(40),
        cost_estimate=pl.CostEstimate(
            flops=2 * hidden.shape[0] * hidden.shape[1] * 512 * count,
            bytes_accessed=(count * 512 + 640) * 1024,
            transcendentals=0,
        ),
        name="adapter_shrink",
    )(base, ids_row, hidden, *downs, *extra)


def expand_kernel(count, final, base_ref, ids_ref, parts_ref, *refs):
    up_refs = refs[:count]
    rest = refs[count:]
    out_ref = rest[-1]
    rank = 16
    sums = jnp.sum(parts_ref[...].astype(f32), axis=0)
    rows = sums.shape[1]
    low = sums[:rank, :].astype(bf16)
    span = up_refs[0].shape[0]
    spread = (
        lax.broadcasted_iota(jnp.int32, (rank, span), 1) % rank
        == lax.broadcasted_iota(jnp.int32, (rank, span), 0)
    )
    tiled = lax.dot_general(
        low,
        spread.astype(f32).astype(bf16),
        (((0,), (0,)), ((), ())),
        preferred_element_type=f32,
    )
    owner = lax.broadcasted_iota(jnp.int32, (rows, span), 1) // rank
    ids = ids_ref[...]
    total = jnp.zeros(out_ref.shape, f32)
    for index in range(count):
        placed = jnp.where(owner == ids - base_ref[index], tiled, 0.0).astype(bf16)
        total = total + jnp.dot(placed, up_refs[index][...], preferred_element_type=f32)
    if not final:
        out_ref[...] = total
        return
    before_ref, mine_ref, theirs_ref = rest[:3]
    widened = (total + before_ref[...]) * adapter_scale
    square = sums[rank : rank + 1, :] + sums[rank + 1 : rank + 2, :]
    inverse = lax.rsqrt(square / 8192.0 + norm_eps)
    column = jnp.transpose(jnp.broadcast_to(inverse, (8, rows)))[:, :1]
    out_ref[...] = ((mine_ref[...] + theirs_ref[...] + widened) * column).astype(out_ref.dtype)


def expand(base, ids_column, parts, ups, final=None):
    count = len(ups)
    rows, columns = ids_column.shape[0], ups[0].shape[1]
    extra = () if final is None else final
    return pl.pallas_call(
        functools.partial(expand_kernel, count, final is not None),
        out_shape=jax.ShapeDtypeStruct((rows, columns), f32 if final is None else bf16),
        in_specs=[SMEM] + [VMEM] * (2 + count + len(extra)),
        out_specs=VMEM,
        compiler_params=params(48),
        cost_estimate=pl.CostEstimate(
            flops=2 * rows * columns * 512 * count,
            bytes_accessed=count * 512 * 768 + rows * columns * 4,
            transcendentals=0,
        ),
        name="adapter_expand",
    )(base, ids_column, parts, *ups, *extra)


def project_kernel(count, place_ref, *refs):
    pieces = refs[:count]
    own_ref, paired_ref, mine_ref, theirs_ref = refs[count:]
    depth = pieces[0].shape[1]
    for index in range(count):
        block = pieces[index][...]
        first = pl.ds(pl.multiple_of(place_ref[index, 0] * depth, depth), depth)
        second = pl.ds(pl.multiple_of(place_ref[index, 1] * depth, depth), depth)
        mine = jnp.dot(block, own_ref[first, :], preferred_element_type=f32)
        theirs = jnp.dot(block, paired_ref[second, :], preferred_element_type=f32)
        if index == 0:
            mine_ref[...] = mine
            theirs_ref[...] = theirs
        else:
            mine_ref[...] += mine
            theirs_ref[...] += theirs


def project(places, pieces, own_weight, paired_weight):
    count = len(pieces)
    rows, columns = pieces[0].shape[0], own_weight.shape[1]
    shape = jax.ShapeDtypeStruct((rows, columns), f32)
    return pl.pallas_call(
        functools.partial(project_kernel, count),
        out_shape=(shape, shape),
        in_specs=[SMEM] + [VMEM] * (count + 2),
        out_specs=(VMEM, VMEM),
        compiler_params=params(48),
        cost_estimate=pl.CostEstimate(
            flops=4 * rows * columns * 512 * count,
            bytes_accessed=18 << 20,
            transcendentals=0,
        ),
        name="base_projection",
    )(places, *pieces, own_weight, paired_weight)


def outgoing_kernel(table_ref, moving_ref, cache_ref, out_ref, sem):
    slots, blocks = table_ref.shape
    size = cache_ref.shape[1]

    def scan(slot, found):
        seen, first, last = found
        hit = moving_ref[slot] == 1
        first = jnp.where(hit & (seen == 0), slot, first)
        last = jnp.where(hit, slot, last)
        return seen + moving_ref[slot], first, last

    zero = jnp.int32(0)
    _, first, last = lax.fori_loop(0, slots, scan, (zero, zero, zero))
    for index, slot in enumerate((first, last)):
        for block in range(blocks):
            pltpu.make_async_copy(
                cache_ref.at[table_ref[slot, block]],
                out_ref.at[index, pl.ds(block * size, size), :],
                sem,
            ).start()
    pltpu.make_async_copy(out_ref, out_ref, sem).wait()


def outgoing(table, moving, cache):
    return pl.pallas_call(
        outgoing_kernel,
        out_shape=jax.ShapeDtypeStruct(
            (MIG_DEV, table.shape[1] * cache.shape[1], cache.shape[2]), cache.dtype
        ),
        in_specs=[SMEM, SMEM, ANY],
        out_specs=VMEM,
        scratch_shapes=[pltpu.SemaphoreType.DMA],
        compiler_params=params(8),
        cost_estimate=pl.CostEstimate(flops=0, bytes_accessed=2 << 20, transcendentals=0),
        name="outgoing_cache",
    )(table, moving, cache)


def attend_kernel(
    table_ref,
    length_ref,
    moving_ref,
    rows_ref,
    cosine_ref,
    sine_ref,
    cache_ref,
    landed_ref,
    out_ref,
    arrived_ref,
    keys_values,
    queries,
    mixed,
    fresh,
    padded,
    sems,
):
    slots, blocks = table_ref.shape
    size = cache_ref.shape[1]
    extent = blocks * size
    reach = extent + NEW_ROWS
    key_columns = KEY_VALUE_HEADS * HEAD_SIZE
    sources, row_count, width = rows_ref.shape
    tokens = row_count // slots
    per_source = width // HEAD_SIZE

    def issue(slot, seen):
        moved = moving_ref[slot]

        @pl.when(moved == 1)
        def _():
            pltpu.make_async_copy(
                landed_ref.at[jnp.minimum(seen, MIG_DEV - 1)],
                keys_values.at[slot, pl.ds(0, extent), :],
                sems.at[slot],
            ).start()

        @pl.when(moved != 1)
        def _():
            for block in range(blocks):
                pltpu.make_async_copy(
                    cache_ref.at[table_ref[slot, block]],
                    keys_values.at[slot, pl.ds(block * size, size), :],
                    sems.at[slot],
                ).start()

        return seen + moved

    lax.fori_loop(0, slots, issue, jnp.int32(0))

    cosine = cosine_ref[...]
    sine = sine_ref[...]
    for source in range(sources):
        for part in range(per_source):
            head = source * per_source + part
            slab = rows_ref[source, :, part * HEAD_SIZE : (part + 1) * HEAD_SIZE]
            if head < QUERY_HEADS + KEY_VALUE_HEADS:
                wide = slab.astype(f32)
                turned = wide * cosine + pltpu.roll(wide, HEAD_SIZE // 2, 1) * sine
            if head < QUERY_HEADS:
                queries[pl.ds(head, row_count, stride=QUERY_HEADS), :] = turned
            else:
                begin = (head - QUERY_HEADS) * HEAD_SIZE
                value = turned.astype(bf16) if head < QUERY_HEADS + KEY_VALUE_HEADS else slab
                fresh[:, begin : begin + HEAD_SIZE] = value

    place = lax.broadcasted_iota(jnp.int32, (slots * NEW_ROWS, row_count), 0)
    source_row = lax.broadcasted_iota(jnp.int32, (slots * NEW_ROWS, row_count), 1)
    token = place % NEW_ROWS
    picked = (token < tokens) & (source_row == (place // NEW_ROWS) * tokens + token)
    padded[...] = jnp.dot(
        picked.astype(f32).astype(bf16), fresh[...], preferred_element_type=f32
    ).astype(bf16)

    arrived_ref[...] = jnp.zeros(arrived_ref.shape, arrived_ref.dtype)

    query_rows = tokens * QUERY_HEADS
    sharing = QUERY_HEADS // KEY_VALUE_HEADS
    group = (lax.broadcasted_iota(jnp.int32, (query_rows, HEAD_SIZE), 0) % QUERY_HEADS) // sharing
    spot = lax.broadcasted_iota(jnp.int32, (query_rows, reach), 1)
    query_token = lax.broadcasted_iota(jnp.int32, (query_rows, reach), 0) // QUERY_HEADS
    fresh_valid = (spot >= extent) & (spot - extent <= query_token)
    scaling = HEAD_SIZE ** (-0.5)

    def step(slot, seen):
        pltpu.make_async_copy(
            keys_values.at[slot, pl.ds(0, extent), :],
            keys_values.at[slot, pl.ds(0, extent), :],
            sems.at[slot],
        ).wait()
        new_rows = padded[pl.ds(pl.multiple_of(slot * NEW_ROWS, NEW_ROWS), NEW_ROWS), :]
        keys_values[slot, extent:reach, :] = new_rows
        begin = pl.multiple_of(slot * query_rows, query_rows)
        query = queries[pl.ds(begin, query_rows), :]
        wide_query = jnp.concatenate(
            [jnp.where(group == head, query, 0.0).astype(bf16) for head in range(KEY_VALUE_HEADS)],
            axis=1,
        )
        scores = (
            lax.dot_general(
                wide_query,
                keys_values[slot, :, :key_columns],
                (((1,), (1,)), ((), ())),
                preferred_element_type=f32,
            )
            * scaling
        )
        length = length_ref[slot]
        valid = (spot < jnp.minimum(length, extent)) | fresh_valid
        scores = jnp.where(valid, scores, -jnp.inf)
        highest = jnp.max(scores, axis=1, keepdims=True)
        powers = jnp.exp(scores - highest)
        weights = (powers / jnp.sum(powers, axis=1, keepdims=True)).astype(bf16)
        values = jnp.dot(weights, keys_values[slot, :, key_columns:], preferred_element_type=f32)
        result = jnp.zeros((query_rows, HEAD_SIZE), f32)
        for head in range(KEY_VALUE_HEADS):
            result = jnp.where(
                group == head, values[:, head * HEAD_SIZE : (head + 1) * HEAD_SIZE], result
            )
        mixed[pl.ds(begin, query_rows), :] = result

        @pl.when(moving_ref[slot] == 1)
        def _():
            target = jnp.minimum(seen, MIG_DEV - 1)
            for left in range(0, 2 * key_columns, 512):
                held = keys_values[slot, :extent, left : left + 512].astype(f32)
                added = padded[
                    pl.ds(pl.multiple_of(slot * NEW_ROWS, NEW_ROWS), NEW_ROWS), left : left + 512
                ].astype(f32)
                at = lax.broadcasted_iota(jnp.int32, (extent, 512), 0)
                kept = jnp.where(at < length, held, 0.0)
                for offset in range(tokens):
                    kept = jnp.where(at == length + offset, added[offset : offset + 1, :], kept)
                arrived_ref[target, :, left : left + 512] = kept.astype(arrived_ref.dtype)

        return seen + moving_ref[slot]

    lax.fori_loop(0, slots, step, jnp.int32(0))

    for head in range(QUERY_HEADS):
        block, inner = head // 2, head % 2
        left = (block // 2) * 256 + inner * HEAD_SIZE
        slab = mixed[pl.ds(head, row_count, stride=QUERY_HEADS), :]
        out_ref[block % 2, :, left : left + HEAD_SIZE] = slab.astype(out_ref.dtype)


def attend(table, lengths, moving, rows, cosine, sine, cache, landed):
    slots = table.shape[0]
    row_count = rows.shape[1]
    extent = table.shape[1] * cache.shape[1]
    tracks = cache.shape[2]
    columns = QUERY_HEADS * HEAD_SIZE
    return pl.pallas_call(
        attend_kernel,
        out_shape=(
            jax.ShapeDtypeStruct((2, row_count, columns // 2), bf16),
            jax.ShapeDtypeStruct(landed.shape, landed.dtype),
        ),
        in_specs=[SMEM, SMEM, SMEM, VMEM, VMEM, VMEM, ANY, ANY],
        out_specs=(VMEM, VMEM),
        scratch_shapes=[
            pltpu.VMEM((slots, extent + NEW_ROWS, tracks), bf16),
            pltpu.VMEM((row_count * QUERY_HEADS, HEAD_SIZE), f32),
            pltpu.VMEM((row_count * QUERY_HEADS, HEAD_SIZE), f32),
            pltpu.VMEM((row_count, tracks), bf16),
            pltpu.VMEM((slots * NEW_ROWS, tracks), bf16),
            pltpu.SemaphoreType.DMA((slots,)),
        ],
        compiler_params=params(40),
        cost_estimate=pl.CostEstimate(
            flops=800_000_000, bytes_accessed=12 << 20, transcendentals=200_000
        ),
        name="paged_attention",
    )(table, lengths, moving, rows, cosine, sine, cache, landed)


def output_kernel(count, place_ref, side_ref, *refs):
    pieces = refs[:count]
    weight_ref, keep_ref, send_ref, stacked = refs[count:]
    height = pieces[0].shape[0]
    for index in range(count):
        begin = pl.multiple_of(place_ref[index] * height, height)
        stacked[pl.ds(begin, height), :] = pieces[index][...]
    half = keep_ref.shape[1]
    tile = 256
    side = side_ref[0]
    for out_ref, part in ((send_ref, 1 - side), (keep_ref, side)):
        for left in range(0, half, tile):
            begin = pl.multiple_of(part * half + left, tile)
            product = jnp.dot(
                stacked[...], weight_ref[:, pl.ds(begin, tile)], preferred_element_type=f32
            )
            out_ref[:, left : left + tile] = product.astype(out_ref.dtype)


def output_projection(places, side, pieces, weight):
    count = len(pieces)
    rows = count * pieces[0].shape[0]
    half = weight.shape[1] // 2
    return pl.pallas_call(
        functools.partial(output_kernel, count),
        out_shape=(
            jax.ShapeDtypeStruct((rows, half), f32),
            jax.ShapeDtypeStruct((rows, half), bf16),
        ),
        in_specs=[SMEM, SMEM] + [VMEM] * (count + 1),
        out_specs=(VMEM, VMEM),
        scratch_shapes=[pltpu.VMEM((rows, weight.shape[0]), bf16)],
        compiler_params=params(40),
        cost_estimate=pl.CostEstimate(
            flops=4 * rows * half * weight.shape[0], bytes_accessed=9 << 20, transcendentals=0
        ),
        name="output_projection",
    )(places, side, *pieces, weight)


def per_device(
    hidden_input,
    input_norm_gain,
    merged_weight,
    output_weight,
    adapter_down,
    adapter_up,
    request_adapter,
    key_value_cache,
    block_table,
    cache_length,
    partner,
    moving,
):
    row_local, fresh_tokens, width = hidden_input.shape
    rows = row_local * fresh_tokens
    core = lax.axis_index("c")
    tensor_rank = lax.axis_index(TENSOR)
    replica_rank = lax.axis_index(REPLICA)
    chips = lax.axis_size(PLANE)
    adapters = adapter_down.shape[0]
    rank = adapter_down.shape[1]

    hidden = hidden_input.reshape(rows, width).astype(f32)
    gain = lax.dynamic_slice_in_dim(input_norm_gain, tensor_rank * width, width).astype(f32)
    gained = (hidden * gain[None, :]).astype(bf16)

    downs = ring_gather(adapter_down.reshape(adapters * rank, width), "z", "h")
    pieces = ring_gather(gained, "x", "l")
    columns = adapter_up.shape[2]
    ups = ring_gather(adapter_up.reshape(adapters * rank, columns), "z", "h")

    squares = jnp.sum(hidden * hidden, axis=-1)[None, :]
    squares = squares + shift(squares, "c", 1)

    by_half = merged_weight.reshape(chips, 2, width, columns)
    leaving = lax.dynamic_index_in_dim(by_half, 1 - core, 1, keepdims=False)
    paired_weight = shift(leaving.reshape(chips * width, columns), "c", 1)

    local_ids = lax.dynamic_slice_in_dim(request_adapter, replica_rank * row_local, row_local, 0)
    ids = jnp.broadcast_to(local_ids[:, None], (row_local, fresh_tokens)).reshape(rows)
    ids_row = ids[None, :]
    ids_column = ids[:, None]
    base = ring_places("z", "h") * adapters
    early = shrink(base[:6], ids_row, gained, downs[:6])
    partial = shrink(base[6:], ids_row, gained, downs[6:], early)
    partial = partial.astype(bf16).astype(f32)
    paired = partial + shift(partial.astype(bf16), "c", 1).astype(f32)
    coarse = lax.reduce_precision(squares, 8, 7)
    fine = squares - coarse
    message = jnp.concatenate(
        [paired.astype(bf16), coarse.astype(bf16), fine.astype(bf16), jnp.zeros((6, rows), bf16)], axis=0
    )
    parts = lax.all_to_all(
        jnp.broadcast_to(message[None], (chips, *message.shape)), PLANE, 0, 0, tiled=True
    )

    spots = ring_places("x", "l")
    places = jnp.stack([spots * 2 + core, spots], axis=1)
    mine, theirs = project(places, pieces, merged_weight, paired_weight)
    other_half = shift(theirs, "c", 1)

    before = expand(base[:6], ids_column, parts, ups[:6])
    projected = expand(base[6:], ids_column, parts, ups[6:], (before, mine, other_half))
    by_request = lax.all_to_all(
        projected.reshape(2 * chips, rows // (2 * chips), columns), TENSOR, 0, 0, tiled=True
    )

    received = outgoing(block_table, moving, key_value_cache)
    pairing = partner[0, tensor_rank]
    for bit, (axis, part) in enumerate((("h", 0), ("z", 0), ("z", 1))):
        swapped = swap_bit(received, axis, part)
        received = jnp.where((pairing >> bit) % 2 == 1, swapped, received)

    half_width = HEAD_SIZE // 2
    frequency = jnp.power(f32(theta_base), -jnp.arange(half_width, dtype=f32) / half_width)
    positions = (
        cache_length[:, None] + jnp.arange(fresh_tokens, dtype=jnp.int32)[None, :]
    ).reshape(-1)
    angles = positions.astype(f32)[:, None] * frequency
    cosine = jnp.cos(angles)
    sine = jnp.sin(angles)
    attended, arrived = attend(
        block_table,
        cache_length,
        moving,
        by_request,
        jnp.concatenate([cosine, cosine], axis=1),
        jnp.concatenate([-sine, sine], axis=1),
        key_value_cache,
        received,
    )

    features = output_weight.shape[1] // chips
    split_weight = jnp.transpose(
        output_weight.reshape(output_weight.shape[0], chips, features), (1, 0, 2)
    )
    split_weight, _ = lax.optimization_barrier((split_weight, pieces[7]))
    stacked_weight = lax.all_to_all(split_weight, PLANE, 0, 0, tiled=True)
    stacked_weight = stacked_weight.reshape(chips * output_weight.shape[0], features)
    kept = lax.dynamic_index_in_dim(attended, core, 0, keepdims=False)
    given = lax.dynamic_index_in_dim(attended, 1 - core, 0, keepdims=False)
    taken = shift(given, "c", 1)
    shard = jnp.where(
        core == 0, jnp.concatenate([kept, taken], axis=0), jnp.concatenate([taken, kept], axis=0)
    )
    blocks = ring_gather(shard, "x", "l")
    keep, send = output_projection(spots, core[None], blocks, stacked_weight)
    summed = keep + shift(send, "c", 1).astype(f32)
    return (summed.astype(bf16).reshape(row_local, fresh_tokens, -1), arrived)


def solution(mesh):
    torus = Mesh(mesh.devices.reshape(4, 2, 4, 2, 2), REPLICA_TENSOR)
    placed = (
        P(REPLICA, None, TENSOR),
        P(),
        P(None, TENSOR),
        P(TENSOR, None),
        P(REPLICA, None, TENSOR),
        P(REPLICA, None, TENSOR),
        P(),
        P(REPLICA_TENSOR, None, None),
        P(REPLICA_TENSOR, None),
        P(REPLICA_TENSOR),
        P(),
        P(REPLICA_TENSOR),
    )
    return jax.shard_map(
        per_device,
        mesh=torus,
        in_specs=placed,
        out_specs=(P(REPLICA, None, TENSOR), P(REPLICA_TENSOR, None, None)),
        check_vma=False,
    )
```
